32 devices in a mesh: dom: 8 (over z, y), cluster: 4 (over x, core).
Axes of the slice: x: 2, y: 2, z: 4, core: 2. Of those that a mesh axis runs over, the one named last changes fastest.
Arguments:
- features: bfloat16 [4, 6144, 512], P('cluster', 'dom'), may hold values from -6 to 6
- stale: bfloat16 [4, 256, 512], P('cluster'), may hold values from -6 to 6
- boundary: int32 [4, 8], P('cluster', 'dom'), may hold values from 0 to 23
- skip: int32 [4, 8], P('cluster'), may hold values 0 or 1
- tile_vals: bfloat16 [4, 256, 32, 128], P('cluster', 'dom'), may hold values from -0.4375 to 0.4375
- tile_row: int32 [4, 256], P('cluster', 'dom'), may hold values from 0 to 5
- tile_src: int32 [4, 256], P('cluster', 'dom'), may hold values from 0 to 9
- tile_count: int32 [4, 8], P('cluster', 'dom'), may hold values from 16 to 32, as said below
- weight: bfloat16 [512, 512], replicated, may hold values from -0.25 to 0.25
- cotangent: bfloat16 [4, 6144, 512], P('cluster', 'dom'), may hold values from -6 to 6
Outputs:
- out_features: bfloat16 [4, 6144, 512], P('cluster', 'dom')
- grad_features: bfloat16 [4, 6144, 512], P('cluster', 'dom')
- grad_weight: float32 [512, 512], P('dom')
The draws below stay inside these ranges and needn't reach their ends.
Inputs may be any that keep to these rules, and one draw needn't show every extreme that they name: `tile_count`: every partition has at least half of its slots live; some partition has all 32 slots live.
All inputs are finite; a program needn't handle non-finite values. No bound on the sum of `skip` on one device may be relied on, other than what follows from the above.
Results may differ from the reference program's by a relative error of at most 0.02.
Values may be sent and summed in bfloat16 or wider, within the bound.
A program may use at most 64 MiB of HBM per device.

```python
import jax
import jax.numpy as jnp
from jax import lax

F = 512
NODE_DEV = 768
BLK = 32
TR = 128
TPD = 32
GROUP_NODES = 6144
CACHE_ROWS = 256
N_DOM = 8
N_CLUSTER = 4


def draw_tile_count(key, part):
    first = jax.random.fold_in(key, 11)
    second = jax.random.fold_in(key, 23)
    third = jax.random.fold_in(key, 37)
    shape = (N_CLUSTER, N_DOM)
    base = jax.random.randint(first, shape, TPD // 2, TPD + 1)
    heavy = jax.random.randint(second, shape, 0, 8) == 0
    counts = jnp.where(heavy, TPD, base)
    where_full = jax.random.randint(third, (), 0, N_CLUSTER * N_DOM)
    flat = counts.reshape(-1)
    flat = jnp.where(jnp.arange(N_CLUSTER * N_DOM) == where_full, TPD, flat)
    return flat.reshape(shape).astype(jnp.int32)


def set_ends(array, rng, low, top_value):
    place = [jax.random.randint(jax.random.fold_in(rng, axis), (), 0, length) for axis, length in enumerate(array.shape)]
    main_axis = array.shape.index(max(array.shape))
    neighbour = place[:main_axis] + [(place[main_axis] + 1) % array.shape[main_axis]] + place[main_axis + 1:]
    return array.at[tuple(place)].set(low).at[tuple(neighbour)].set(top_value)


def block_levels(key, dims, cuts, low, top_value):
    level = 1.0
    for axis_at, shards_of in cuts:
        steps = jax.random.uniform(jax.random.fold_in(jax.random.fold_in(key, 6), axis_at), (shards_of,), jnp.float32, low / len(cuts), top_value / len(cuts))
        level = level * jnp.repeat(jnp.exp(steps), dims[axis_at] // shards_of).reshape((-1,) + (1,) * (len(dims) - 1 - axis_at))
    return level


def centred(stream_key, extent, scale, bound, cuts=(), kind=jnp.bfloat16):
    array = scale * jax.random.normal(stream_key, extent, jnp.float32)
    if cuts:
        array = array * block_levels(stream_key, extent, cuts, -0.22, 0.18)
    return jnp.clip(array, -bound, bound).astype(kind)


def setup_inputs(seed: int = 0) -> dict:
    splits = jax.random.split(jax.random.key(seed), 11)
    features = centred(splits[0], (N_CLUSTER, GROUP_NODES, F), 1.0, 6.0, ((0, 4), (1, 8)))
    stale = centred(splits[1], (N_CLUSTER, CACHE_ROWS, F), 1.0, 6.0, ((0, 4),))
    boundary = set_ends(jax.random.randint(splits[2], (N_CLUSTER, N_DOM), 0, NODE_DEV // BLK), jax.random.fold_in(splits[2], 1), 0, (NODE_DEV // BLK) - 1).astype(jnp.int32)
    skip = set_ends((jax.random.randint(splits[3], (N_CLUSTER, N_DOM), 0, 4) < 1).astype(jnp.int32), jax.random.fold_in(splits[3], 1), 0, 1)
    tile_vals = centred(splits[4], (N_CLUSTER, N_DOM * TPD, BLK, TR), (BLK * TPD * TR // NODE_DEV) ** -0.5, 0.4375, ((0, 4), (1, 8)))
    tile_row = set_ends(jax.random.randint(splits[5], (N_CLUSTER, N_DOM * TPD), 0, NODE_DEV // TR), jax.random.fold_in(splits[5], 1), 0, (NODE_DEV // TR) - 1).astype(jnp.int32)
    tile_src = set_ends(jax.random.randint(splits[6], (N_CLUSTER, N_DOM * TPD), 0, N_DOM + 2), jax.random.fold_in(splits[6], 1), 0, (N_DOM + 2) - 1).astype(jnp.int32)
    tile_count = draw_tile_count(jax.random.fold_in(splits[10], 71), 0)
    weight = centred(splits[8], (F, F), F ** -0.5, 0.25)
    cotangent = centred(splits[9], (N_CLUSTER, GROUP_NODES, F), 1.0, 6.0, ((0, 4), (1, 8)))
    return dict(features=features, stale=stale, boundary=boundary, skip=skip, tile_vals=tile_vals, tile_row=tile_row, tile_src=tile_src, tile_count=tile_count, weight=weight, cotangent=cotangent)


def silu_parts(value):
    sig = jax.nn.sigmoid(value)
    return value * sig, sig * (1.0 + value * (1.0 - sig))


def reference(features, stale, boundary, skip, tile_vals, tile_row, tile_src, tile_count, weight, cotangent):
    n_clu = N_CLUSTER
    n_part = N_DOM
    n_blocks = NODE_DEV // BLK
    n_rowblk = NODE_DEV // TR
    blocks = features.reshape(n_clu, n_part, n_blocks, BLK, F)
    picks = boundary.astype(jnp.int32)[:, :, None, None, None]
    exported = jnp.take_along_axis(blocks, picks, axis=2)[:, :, 0]
    cached = stale.reshape(n_clu, n_part, BLK, F)
    fresh = jnp.where((skip == 1)[:, :, None, None], cached, exported)
    lower = jnp.roll(exported, 1, axis=0)
    upper = jnp.roll(exported, -1, axis=0)
    tile_blocks = tile_vals.reshape(n_clu * n_part, TPD, BLK, TR)
    rows = tile_row.reshape(n_clu * n_part, TPD)
    srcs = tile_src.reshape(n_clu * n_part, TPD)
    counts = tile_count.reshape(n_clu * n_part)
    feats = features.reshape(n_clu * n_part, NODE_DEV, F)
    cots = cotangent.reshape(n_clu * n_part, NODE_DEV, F)

    def visit(carry, index):
        wsum, gsum = carry
        clu = index // n_part
        part = index % n_part
        table = jnp.concatenate([fresh[clu], lower[clu, part][None], upper[clu, part][None]], axis=0)
        active_mask = (jnp.arange(TPD, dtype=jnp.int32) < counts[index]).astype(jnp.float32)
        local_tile_block = tile_blocks[index].astype(jnp.float32)
        selected_block = jnp.take(table, srcs[index], axis=0).astype(jnp.float32)
        contribution = jnp.einsum("wnz,wnx->wzx", local_tile_block, selected_block) * active_mask[:, None, None]
        row_onehot_mask = (rows[index][:, None] == jnp.arange(n_rowblk, dtype=jnp.int32)[None, :]).astype(jnp.float32)
        row_onehot_mask = row_onehot_mask * active_mask[:, None]
        aggregate_block_list = jnp.einsum("xn,xij->nij", row_onehot_mask, contribution, precision=lax.Precision.HIGHEST)
        agg = (feats[index].astype(jnp.float32) + aggregate_block_list.reshape(NODE_DEV, F)).astype(jnp.bfloat16)
        zval = jnp.dot(agg, weight, preferred_element_type=jnp.float32)
        act, slope = silu_parts(zval)
        dz = (cots[index].astype(jnp.float32) * slope).astype(jnp.bfloat16)
        wsum = wsum + lax.dot_general(agg, dz, (((0,), (0,)), ((), ())), preferred_element_type=jnp.float32)
        dagg = lax.dot_general(dz, weight, (((1,), (1,)), ((), ())), preferred_element_type=jnp.float32).astype(jnp.bfloat16)
        selected_rows = jnp.take(dagg.reshape(n_rowblk, TR, F), rows[index], axis=0).astype(jnp.float32)
        selected_gradient = jnp.einsum("dck,dkn->dcn", local_tile_block, selected_rows) * active_mask[:, None, None]
        src_hot = (srcs[index][:, None] == jnp.arange(n_part + 2, dtype=jnp.int32)[None, :]).astype(jnp.float32)
        dsrc = jnp.einsum("ts,tbf->sbf", src_hot, selected_gradient, precision=lax.Precision.HIGHEST)
        keep = (1 - skip[clu]).astype(jnp.float32)
        gsum = gsum.at[clu].add(dsrc[:n_part] * keep[:, None, None])
        return (wsum, gsum), (act.astype(jnp.bfloat16), dagg, dsrc[n_part], dsrc[n_part + 1])

    init = (jnp.zeros((F, F), jnp.float32), jnp.zeros((n_clu, n_part, BLK, F), jnp.float32))
    (wsum, gsum), (outs, daggs, low_grads, up_grads) = lax.scan(visit, init, jnp.arange(n_clu * n_part, dtype=jnp.int32))
    low_grads = low_grads.reshape(n_clu, n_part, BLK, F)
    up_grads = up_grads.reshape(n_clu, n_part, BLK, F)
    bgrad = gsum + jnp.roll(low_grads, -1, axis=0) + jnp.roll(up_grads, 1, axis=0)
    hot = (boundary[:, :, None] == jnp.arange(n_blocks, dtype=jnp.int32)[None, None, :]).astype(jnp.float32)
    full = daggs.reshape(n_clu, n_part, n_blocks, BLK, F).astype(jnp.float32)
    full = full + hot[:, :, :, None, None] * bgrad[:, :, None]
    out_features = outs.reshape(n_clu, n_part * NODE_DEV, F)
    grad_features = full.reshape(n_clu, n_part * NODE_DEV, F).astype(jnp.bfloat16)
    return out_features, grad_features, wsum
```

```python
import functools

import jax
import jax.numpy as jnp
from jax import lax
from jax.experimental import pallas as pl
from jax.experimental.pallas import tpu as pltpu
from jax.sharding import PartitionSpec as P

MESH = pl.DeviceIdType.MESH
F32 = jnp.float32
BF16 = jnp.bfloat16


def dot(a, b, da, db):
    return lax.dot_general(a, b, (((da,), (db,)), ((), ())), preferred_element_type=F32)


def iota(shape, axis):
    return lax.broadcasted_iota(jnp.int32, shape, axis)


def kernel(
    doms,
    clusters,
    bnd,
    skip,
    trow,
    tsrc,
    tcnt,
    feats_h,
    tiles_h,
    stale_h,
    weight_h,
    cot_h,
    out,
    gfeat,
    gw,
    feats,
    tiles,
    stale,
    weight,
    cot,
    own,
    gath,
    table,
    spread,
    picks,
    adj,
    agg,
    dz,
    dagg,
    half_out,
    half_in,
    pair,
    pair_in,
    bg_out,
    bg_in,
    quarter,
    quarter_in,
    load_sem,
    ag_send,
    ag_recv,
    half_send,
    half_recv,
    pair_send,
    pair_recv,
    bg_send,
    bg_recv,
    q_send,
    q_recv,
):
    me = lax.axis_index("dom")
    mine = lax.axis_index("cluster")
    parity = lax.rem(mine, 2)
    nodes, width = feats.shape
    slots, blk, tile_rows = tiles.shape
    row_blocks = nodes // tile_rows
    half = width // 2
    share = width // doms

    def dom_at(k):
        return {"dom": lax.rem(me + k + doms, doms)}

    def cluster_at(k):
        return {"cluster": lax.rem(mine + k + clusters, clusters)}

    loads = []
    for i, (src, dst) in enumerate(
        ((feats_h, feats), (tiles_h, tiles), (stale_h, stale), (weight_h, weight), (cot_h, cot))
    ):
        loads.append(pltpu.make_async_copy(src, dst, load_sem.at[i]))
        loads[-1].start()

    barrier = pltpu.get_barrier_semaphore()
    for k in range(1, doms):
        pl.semaphore_signal(barrier, inc=1, device_id=dom_at(k), device_id_type=MESH)
    for k in range(1, clusters):
        pl.semaphore_signal(barrier, inc=1, device_id=cluster_at(k), device_id_type=MESH)

    loads[0].wait()
    exported = iota((blk, nodes), 1) - iota((blk, nodes), 0) == bnd[0, 0] * blk
    own[...] = dot(jnp.where(exported, 1.0, 0.0).astype(BF16), feats[...], 1, 0).astype(BF16)
    pl.semaphore_wait(barrier, doms - 1 + clusters - 1)

    def remote(src, dst, send, recv, to):
        copy = pltpu.make_async_remote_copy(
            src_ref=src, dst_ref=dst, send_sem=send, recv_sem=recv, device_id=to, device_id_type=MESH
        )
        copy.start()
        return copy

    gathers = []
    for k in range(1, doms):
        gathers.append(
            remote(own, gath.at[k], ag_send.at[k], ag_recv.at[k], dom_at(k))
        )
    for k, by in ((doms, 1), (doms + 1, -1)):
        gathers.append(
            remote(own, gath.at[k], ag_send.at[k], ag_recv.at[k], cluster_at(by))
        )

    loads[1].wait()
    sources = (doms + 2) * blk
    offset = iota((blk, sources), 1) - iota((blk, sources), 0)
    row_block = iota((blk, nodes), 1) // tile_rows
    for t in range(slots):
        at = slice(t * blk, (t + 1) * blk)
        picks[at, :] = jnp.where(offset == tsrc[0, t] * blk, 1.0, 0.0).astype(BF16)
        row = trow[0, t] + nodes * jnp.maximum(t + 1 - tcnt[0, 0], 0)
        block = jnp.concatenate([tiles[t].astype(F32)] * row_blocks, axis=1)
        spread[at, :] = jnp.where(row_block == row, block, 0.0).astype(BF16)
    adj[...] = dot(picks[...], spread[...], 0, 0).astype(BF16)

    loads[2].wait()
    loads[3].wait()
    loads[4].wait()
    one = jnp.ones((blk, width), jnp.int32)

    def block_of(k):
        source = lax.rem(me - k + doms, doms) if k < doms else k
        return source, pl.ds(pl.multiple_of(source * blk, blk), blk)

    for k in range(doms + 2):
        if k > 0:
            gathers[k - 1].wait_recv()
        fresh = own[...] if k == 0 else gath[k]
        source, at = block_of(k)
        if k < doms:
            cached = one == skip[0, source]
            fresh = jnp.where(cached, stale[at, :].astype(F32), fresh.astype(F32)).astype(BF16)
        table[at, :] = fresh

    chunk = 2 * tile_rows
    for r in range(0, nodes, chunk):
        rows = slice(r, r + chunk)
        total = feats[rows, :].astype(F32) + dot(adj[:, rows], table[...], 0, 0)
        total = total.astype(BF16)
        agg[rows, :] = total
        z = dot(total, weight[...], 1, 0)
        sig = 1.0 / (1.0 + jnp.exp(-z))
        act = z * sig
        out[rows, :] = act.astype(BF16)
        dz[rows, :] = (cot[rows, :].astype(F32) * (sig * (1.0 + z * (1.0 - sig)))).astype(BF16)

    def half_at(which):
        return pl.ds(pl.multiple_of(which * half, half), half)

    half_out[...] = dot(agg[...], dz[:, half_at(1 - parity)], 0, 0).astype(BF16)
    partner = {"cluster": mine + 1 - 2 * parity}
    halves = remote(half_out, half_in, half_send.at[0], half_recv.at[0], partner)

    for r in range(0, nodes, chunk):
        rows = slice(r, r + chunk)
        dagg[rows, :] = dot(dz[rows, :], weight[...], 1, 1).astype(BF16)
    dsrc = dot(adj[...], dagg[...], 1, 0)
    for source in range(doms + 2):
        at = slice(source * blk, (source + 1) * blk)
        grad = dsrc[at, :]
        if source < doms:
            grad = jnp.where(one == skip[0, source], 0.0, grad)
        bg_out[at, :] = grad.astype(BF16)
    blocks = []
    for k in range(1, doms + 2):
        to = dom_at(-k) if k < doms else cluster_at(-1 if k == doms else 1)
        blocks.append(
            remote(bg_out.at[block_of(k)[1]], bg_in.at[k], bg_send.at[k], bg_recv.at[k], to)
        )

    wsum = dot(agg[...], dz[:, half_at(parity)], 0, 0)
    halves.wait_recv()
    wsum = wsum + half_in[...].astype(F32)
    pair[...] = wsum.astype(BF16)

    def share_at(k):
        part = lax.rem(me + k + doms, doms)
        return pl.ds(pl.multiple_of(part * share, share), share)

    pairs = []
    for k in range(1, doms):
        pairs.append(
            remote(pair.at[share_at(k)], pair_in.at[k], pair_send.at[k], pair_recv.at[k], dom_at(k))
        )

    bgrad = bg_out[block_of(0)[1], :].astype(F32)
    for k in range(1, doms + 2):
        blocks[k - 1].wait_recv()
        bgrad = bgrad + bg_in[k].astype(F32)
    for b in range(nodes // blk):
        rows = slice(b * blk, (b + 1) * blk)
        here = jnp.where(one * b == bnd[0, 0], bgrad, 0.0)
        gfeat[rows, :] = (dagg[rows, :].astype(F32) + here).astype(BF16)

    rsum = pair[share_at(0), :].astype(F32)
    for k in range(1, doms):
        pairs[k - 1].wait_recv()
        rsum = rsum + pair_in[k].astype(F32)
    quarter[...] = rsum.astype(BF16)
    quarters = []
    for k in range(1, clusters):
        quarters.append(
            remote(quarter, quarter_in.at[k], q_send.at[k], q_recv.at[k], cluster_at(k))
        )
    same = quarter[...].astype(F32)
    other = jnp.zeros_like(same)
    for k in range(1, clusters):
        quarters[k - 1].wait_recv()
        if k % 2 == 0:
            same = same + quarter_in[k].astype(F32)
        else:
            other = other + quarter_in[k].astype(F32)
    gw[:, half_at(parity)] = same
    gw[:, half_at(1 - parity)] = other

    for copy in gathers + [halves] + blocks + pairs + quarters:
        copy.wait_send()


def per_device(
    doms,
    clusters,
    features,
    stale,
    boundary,
    skip,
    tile_vals,
    tile_row,
    tile_src,
    tile_count,
    weight,
    cotangent,
):
    _, nodes, width = features.shape
    _, slots, blk, tile_rows = tile_vals.shape
    half, share = width // 2, width // doms
    smem = pl.BlockSpec(memory_space=pltpu.SMEM)
    vmem = pl.BlockSpec(memory_space=pltpu.VMEM)
    hbm = pl.BlockSpec(memory_space=pl.ANY)
    dma = pltpu.SemaphoreType.DMA
    out, gfeat, gw = pl.pallas_call(
        functools.partial(kernel, doms, clusters),
        out_shape=(
            jax.ShapeDtypeStruct((nodes, width), BF16),
            jax.ShapeDtypeStruct((nodes, width), BF16),
            jax.ShapeDtypeStruct((share, width), F32),
        ),
        in_specs=[smem] * 5 + [hbm] * 5,
        out_specs=(vmem, vmem, vmem),
        scratch_shapes=[
            pltpu.VMEM((nodes, width), BF16),
            pltpu.VMEM((slots, blk, tile_rows), BF16),
            pltpu.VMEM((doms * blk, width), BF16),
            pltpu.VMEM((width, width), BF16),
            pltpu.VMEM((nodes, width), BF16),
            pltpu.VMEM((blk, width), BF16),
            pltpu.VMEM((doms + 2, blk, width), BF16),
            pltpu.VMEM(((doms + 2) * blk, width), BF16),
            pltpu.VMEM((slots * blk, nodes), BF16),
            pltpu.VMEM((slots * blk, (doms + 2) * blk), BF16),
            pltpu.VMEM(((doms + 2) * blk, nodes), BF16),
            pltpu.VMEM((nodes, width), BF16),
            pltpu.VMEM((nodes, width), BF16),
            pltpu.VMEM((nodes, width), BF16),
            pltpu.VMEM((width, half), BF16),
            pltpu.VMEM((width, half), BF16),
            pltpu.VMEM((width, half), BF16),
            pltpu.VMEM((doms, share, half), BF16),
            pltpu.VMEM(((doms + 2) * blk, width), BF16),
            pltpu.VMEM((doms + 2, blk, width), BF16),
            pltpu.VMEM((share, half), BF16),
            pltpu.VMEM((clusters, share, half), BF16),
            dma((5,)),
            dma((doms + 2,)),
            dma((doms + 2,)),
            dma((1,)),
            dma((1,)),
            dma((doms,)),
            dma((doms,)),
            dma((doms + 2,)),
            dma((doms + 2,)),
            dma((clusters,)),
            dma((clusters,)),
        ],
        compiler_params=pltpu.CompilerParams(
            collective_id=0, has_side_effects=True, vmem_limit_bytes=40 * 2**20
        ),
    )(
        boundary,
        skip,
        tile_row,
        tile_src,
        tile_count,
        features[0],
        tile_vals[0],
        stale[0],
        weight,
        cotangent[0],
    )
    return (out[None], gfeat[None], gw)


def solution(mesh):
    return jax.shard_map(
        functools.partial(per_device, mesh.shape["dom"], mesh.shape["cluster"]),
        mesh=mesh,
        in_specs=(
            P("cluster", "dom", None),
            P("cluster", None, None),
            P("cluster", "dom"),
            P("cluster", None),
            P("cluster", "dom", None, None),
            P("cluster", "dom"),
            P("cluster", "dom"),
            P("cluster", "dom"),
            P(),
            P("cluster", "dom", None),
        ),
        out_specs=(P("cluster", "dom", None), P("cluster", "dom", None), P("dom", None)),
        check_vma=False,
    )
```

```python
import functools

import jax
import jax.numpy as jnp
from jax import lax
from jax.experimental import pallas as pl
from jax.experimental.pallas import tpu as pltpu
from jax.sharding import PartitionSpec as P

MESH = pl.DeviceIdType.MESH
F32 = jnp.float32
BF16 = jnp.bfloat16


def dot(a, b, da, db):
    return lax.dot_general(a, b, (((da,), (db,)), ((), ())), preferred_element_type=F32)


def iota(shape, axis):
    return lax.broadcasted_iota(jnp.int32, shape, axis)


def kernel(
    doms,
    clusters,
    bnd,
    skip,
    trow,
    tsrc,
    tcnt,
    feats_h,
    tiles_h,
    stale_h,
    weight_h,
    cot_h,
    out,
    gfeat,
    gw,
    feats,
    tiles,
    stale,
    weight,
    cot,
    own,
    gath,
    table,
    spread,
    picks,
    adj,
    agg,
    dz,
    dagg,
    half_out,
    half_in,
    pair,
    pair_in,
    bg_out,
    bg_in,
    quarter,
    quarter_in,
    load_sem,
    ag_send,
    ag_recv,
    half_send,
    half_recv,
    pair_send,
    pair_recv,
    bg_send,
    bg_recv,
    q_send,
    q_recv,
):
    me = lax.axis_index("dom")
    mine = lax.axis_index("cluster")
    parity = lax.rem(mine, 2)
    nodes, width = feats.shape
    slots, blk, tile_rows = tiles.shape
    row_blocks = nodes // tile_rows
    half = width // 2
    share = width // doms

    def dom_at(k):
        return {"dom": lax.rem(me + k + doms, doms)}

    def cluster_at(k):
        return {"cluster": lax.rem(mine + k + clusters, clusters)}

    loads = []
    for i, (src, dst) in enumerate(
        ((feats_h, feats), (tiles_h, tiles), (stale_h, stale), (weight_h, weight), (cot_h, cot))
    ):
        loads.append(pltpu.make_async_copy(src, dst, load_sem.at[i]))
        loads[-1].start()

    barrier = pltpu.get_barrier_semaphore()
    for k in range(1, doms):
        pl.semaphore_signal(barrier, inc=1, device_id=dom_at(k), device_id_type=MESH)
    for k in range(1, clusters):
        pl.semaphore_signal(barrier, inc=1, device_id=cluster_at(k), device_id_type=MESH)

    loads[0].wait()
    exported = iota((blk, nodes), 1) - iota((blk, nodes), 0) == bnd[0, 0] * blk
    own[...] = dot(jnp.where(exported, 1.0, 0.0).astype(BF16), feats[...], 1, 0).astype(BF16)
    pl.semaphore_wait(barrier, doms - 1 + clusters - 1)

    def remote(src, dst, send, recv, to):
        copy = pltpu.make_async_remote_copy(
            src_ref=src, dst_ref=dst, send_sem=send, recv_sem=recv, device_id=to, device_id_type=MESH
        )
        copy.start()
        return copy

    gathers = {}

    def gather(src, slot, to):
        return remote(src, gath.at[slot], ag_send.at[slot], ag_recv.at[slot], to)

    aside = 1 - 2 * lax.rem(me, 2)
    pair_to = {"dom": me + aside}

    def forward(k):
        slot = lax.rem(k + aside + doms, doms)
        src = own if k == 0 else gath.at[k]
        return gather(src, slot, pair_to)

    near = list(range(2, doms, 2))
    for k in near:
        gathers[k] = gather(own, k, dom_at(k))
    forwards = [forward(0)]
    for k, by in ((doms, 1), (doms + 1, -1)):
        gathers[k] = gather(own, k, cluster_at(by))

    loads[1].wait()
    sources = (doms + 2) * blk
    offset = iota((blk, sources), 1) - iota((blk, sources), 0)
    row_block = iota((blk, nodes), 1) // tile_rows
    for t in range(slots):
        at = slice(t * blk, (t + 1) * blk)
        picks[at, :] = jnp.where(offset == tsrc[0, t] * blk, 1.0, 0.0).astype(BF16)
        row = trow[0, t] + nodes * jnp.maximum(t + 1 - tcnt[0, 0], 0)
        block = jnp.concatenate([tiles[t].astype(F32)] * row_blocks, axis=1)
        spread[at, :] = jnp.where(row_block == row, block, 0.0).astype(BF16)
    for k in sorted(near, key=lambda k: min(k, doms - k)):
        gathers[k].wait_recv()
        forwards.append(forward(k))
    adj[...] = dot(picks[...], spread[...], 0, 0).astype(BF16)

    loads[2].wait()
    loads[3].wait()
    loads[4].wait()
    one = jnp.ones((blk, width), jnp.int32)

    def block_of(k):
        source = lax.rem(me - k + doms, doms) if k < doms else k
        return source, pl.ds(pl.multiple_of(source * blk, blk), blk)

    for k in range(doms + 2):
        if k >= doms:
            gathers[k].wait_recv()
        elif k % 2 == 1:
            pltpu.make_async_copy(gath.at[k], gath.at[k], ag_recv.at[k]).wait()
        fresh = own[...] if k == 0 else gath[k]
        source, at = block_of(k)
        if k < doms:
            cached = one == skip[0, source]
            fresh = jnp.where(cached, stale[at, :].astype(F32), fresh.astype(F32)).astype(BF16)
        table[at, :] = fresh

    chunk = 2 * tile_rows
    for r in range(0, nodes, chunk):
        rows = slice(r, r + chunk)
        total = feats[rows, :].astype(F32) + dot(adj[:, rows], table[...], 0, 0)
        total = total.astype(BF16)
        agg[rows, :] = total
        z = dot(total, weight[...], 1, 0)
        sig = 1.0 / (1.0 + jnp.exp(-z))
        act = z * sig
        out[rows, :] = act.astype(BF16)
        dz[rows, :] = (cot[rows, :].astype(F32) * (sig * (1.0 + z * (1.0 - sig)))).astype(BF16)

    def half_at(which):
        return pl.ds(pl.multiple_of(which * half, half), half)

    half_out[...] = dot(agg[...], dz[:, half_at(1 - parity)], 0, 0).astype(BF16)
    partner = {"cluster": mine + 1 - 2 * parity}
    halves = remote(half_out, half_in, half_send.at[0], half_recv.at[0], partner)

    wsum = dot(agg[...], dz[:, half_at(parity)], 0, 0)
    halves.wait_recv()
    wsum = wsum + half_in[...].astype(F32)
    pair[...] = wsum.astype(BF16)

    def share_at(k):
        part = lax.rem(me + k + doms, doms)
        return pl.ds(pl.multiple_of(part * share, share), share)

    pairs = []
    for k in range(1, doms):
        pairs.append(
            remote(pair.at[share_at(k)], pair_in.at[k], pair_send.at[k], pair_recv.at[k], dom_at(k))
        )

    for r in range(0, nodes, chunk):
        rows = slice(r, r + chunk)
        dagg[rows, :] = dot(dz[rows, :], weight[...], 1, 1).astype(BF16)
    dsrc = dot(adj[...], dagg[...], 1, 0)
    for source in range(doms + 2):
        at = slice(source * blk, (source + 1) * blk)
        grad = dsrc[at, :]
        if source < doms:
            grad = jnp.where(one == skip[0, source], 0.0, grad)
        bg_out[at, :] = grad.astype(BF16)
    blocks = []
    for k in range(1, doms + 2):
        to = dom_at(-k) if k < doms else cluster_at(-1 if k == doms else 1)
        blocks.append(
            remote(bg_out.at[block_of(k)[1]], bg_in.at[k], bg_send.at[k], bg_recv.at[k], to)
        )

    rsum = pair[share_at(0), :].astype(F32)
    for k in range(1, doms):
        pairs[k - 1].wait_recv()
        rsum = rsum + pair_in[k].astype(F32)
    quarter[...] = rsum.astype(BF16)
    quarters = []
    for k in range(1, clusters):
        quarters.append(
            remote(quarter, quarter_in.at[k], q_send.at[k], q_recv.at[k], cluster_at(k))
        )
    bgrad = bg_out[block_of(0)[1], :].astype(F32)
    for k in range(1, doms + 2):
        blocks[k - 1].wait_recv()
        bgrad = bgrad + bg_in[k].astype(F32)
    for b in range(nodes // blk):
        rows = slice(b * blk, (b + 1) * blk)
        here = jnp.where(one * b == bnd[0, 0], bgrad, 0.0)
        gfeat[rows, :] = (dagg[rows, :].astype(F32) + here).astype(BF16)

    same = quarter[...].astype(F32)
    other = jnp.zeros_like(same)
    for k in range(1, clusters):
        quarters[k - 1].wait_recv()
        if k % 2 == 0:
            same = same + quarter_in[k].astype(F32)
        else:
            other = other + quarter_in[k].astype(F32)
    gw[:, half_at(parity)] = same
    gw[:, half_at(1 - parity)] = other

    for copy in list(gathers.values()) + forwards + [halves] + blocks + pairs + quarters:
        copy.wait_send()


def per_device(
    doms,
    clusters,
    features,
    stale,
    boundary,
    skip,
    tile_vals,
    tile_row,
    tile_src,
    tile_count,
    weight,
    cotangent,
):
    _, nodes, width = features.shape
    _, slots, blk, tile_rows = tile_vals.shape
    half, share = width // 2, width // doms
    smem = pl.BlockSpec(memory_space=pltpu.SMEM)
    vmem = pl.BlockSpec(memory_space=pltpu.VMEM)
    hbm = pl.BlockSpec(memory_space=pltpu.HBM)
    dma = pltpu.SemaphoreType.DMA
    out, gfeat, gw = pl.pallas_call(
        functools.partial(kernel, doms, clusters),
        out_shape=(
            jax.ShapeDtypeStruct((nodes, width), BF16),
            jax.ShapeDtypeStruct((nodes, width), BF16),
            jax.ShapeDtypeStruct((share, width), F32),
        ),
        in_specs=[smem] * 5 + [hbm] * 5,
        out_specs=(vmem, vmem, vmem),
        scratch_shapes=[
            pltpu.VMEM((nodes, width), BF16),
            pltpu.VMEM((slots, blk, tile_rows), BF16),
            pltpu.VMEM((doms * blk, width), BF16),
            pltpu.VMEM((width, width), BF16),
            pltpu.VMEM((nodes, width), BF16),
            pltpu.VMEM((blk, width), BF16),
            pltpu.VMEM((doms + 2, blk, width), BF16),
            pltpu.VMEM(((doms + 2) * blk, width), BF16),
            pltpu.VMEM((slots * blk, nodes), BF16),
            pltpu.VMEM((slots * blk, (doms + 2) * blk), BF16),
            pltpu.VMEM(((doms + 2) * blk, nodes), BF16),
            pltpu.VMEM((nodes, width), BF16),
            pltpu.VMEM((nodes, width), BF16),
            pltpu.VMEM((nodes, width), BF16),
            pltpu.VMEM((width, half), BF16),
            pltpu.VMEM((width, half), BF16),
            pltpu.VMEM((width, half), BF16),
            pltpu.VMEM((doms, share, half), BF16),
            pltpu.VMEM(((doms + 2) * blk, width), BF16),
            pltpu.VMEM((doms + 2, blk, width), BF16),
            pltpu.VMEM((share, half), BF16),
            pltpu.VMEM((clusters, share, half), BF16),
            dma((5,)),
            dma((doms + 2,)),
            dma((doms + 2,)),
            dma((1,)),
            dma((1,)),
            dma((doms,)),
            dma((doms,)),
            dma((doms + 2,)),
            dma((doms + 2,)),
            dma((clusters,)),
            dma((clusters,)),
        ],
        compiler_params=pltpu.CompilerParams(
            collective_id=0, has_side_effects=True, vmem_limit_bytes=62 * 2**20
        ),
    )(
        boundary,
        skip,
        tile_row,
        tile_src,
        tile_count,
        features[0],
        tile_vals[0],
        stale[0],
        weight,
        cotangent[0],
    )
    return (out[None], gfeat[None], gw)


def solution(mesh):
    return jax.shard_map(
        functools.partial(per_device, mesh.shape["dom"], mesh.shape["cluster"]),
        mesh=mesh,
        in_specs=(
            P("cluster", "dom", None),
            P("cluster", None, None),
            P("cluster", "dom"),
            P("cluster", None),
            P("cluster", "dom", None, None),
            P("cluster", "dom"),
            P("cluster", "dom"),
            P("cluster", "dom"),
            P(),
            P("cluster", "dom", None),
        ),
        out_specs=(P("cluster", "dom", None), P("cluster", "dom", None), P("dom", None)),
        check_vma=False,
    )
```
